32 devices in a mesh: dp: 16 (over z, y, x), tensor: 2 (over core).
Axes of the slice: x: 2, y: 2, z: 4, core: 2. Of those that a mesh axis runs over, the one named last changes fastest.
Arguments:
- images: bfloat16 [2, 96, 197, 768], P(None, 'dp'), may hold values from -6 to 6
- live_images: int32 [2, 16], P(None, 'dp'), may hold values from 1 to 6, as said below
- ln1_gain: bfloat16 [768], P('dp'), may hold values from 0.5 to 1.5
- ln1_bias: bfloat16 [768], P('dp'), may hold values from -3 to 3
- qkv_weight: bfloat16 [768, 3, 768], P('dp', None, 'tensor'), may hold values from -1 to 1
- qkv_bias: bfloat16 [2, 768], P(None, ('tensor', 'dp')), may hold values from -3 to 3
- proj_weight: bfloat16 [768, 768], P('tensor', 'dp'), may hold values from -0.875 to 0.875
- proj_bias: bfloat16 [768], P('dp'), may hold values from -3 to 3
- ln2_gain: bfloat16 [768], P('dp'), may hold values from 0.5 to 1.5
- ln2_bias: bfloat16 [768], P('dp'), may hold values from -3 to 3
- fc1_weight: bfloat16 [768, 3072], P('dp', 'tensor'), may hold values from -0.21875 to 0.21875
- fc1_bias: bfloat16 [3072], P(('tensor', 'dp')), may hold values from -3 to 3
- fc2_weight: bfloat16 [3072, 768], P('tensor', 'dp'), may hold values from -0.109375 to 0.109375
- fc2_bias: bfloat16 [768], P('dp'), may hold values from -3 to 3
- cotangent: bfloat16 [2, 96, 197, 768], P(None, 'dp'), may hold values from -6 to 6
Outputs:
- activations: bfloat16 [2, 96, 197, 768], P(None, 'dp')
- input_grad: float32 [2, 96, 197, 768], P(None, 'dp')
- grad_ln1_gain: float32 [768], P('dp')
- grad_ln1_bias: float32 [768], P('dp')
- grad_qkv_weight: float32 [768, 3, 768], P('dp', None, 'tensor')
- grad_qkv_bias: float32 [2, 768], P(None, ('tensor', 'dp'))
- grad_proj_weight: float32 [768, 768], P('tensor', 'dp')
- grad_proj_bias: float32 [768], P('dp')
- grad_ln2_gain: float32 [768], P('dp')
- grad_ln2_bias: float32 [768], P('dp')
- grad_fc1_weight: float32 [768, 3072], P('dp', 'tensor')
- grad_fc1_bias: float32 [3072], P(('tensor', 'dp'))
- grad_fc2_weight: float32 [3072, 768], P('tensor', 'dp')
- grad_fc2_bias: float32 [768], P('dp')
The draws below stay inside these ranges and needn't reach their ends.
Inputs may be any that keep to these rules, and one draw needn't show every extreme that they name: live_images[b, r] is how many of data rank r's 6 slots of micro-batch b hold live images, slots 0 upward; in each micro-batch some rank has all 6 live and some rank one.
All inputs are finite; a program needn't handle non-finite values.
Results may differ from the reference program's by a relative error of at most 0.015.
Values may be sent and summed in bfloat16 or wider, within the bound.
No kernel may reach another device: no remote copies, remote signals or barrier semaphores. Data moves between devices by JAX's collectives and lax.ppermute only.
A program may use at most 256 MiB of HBM per device.

```python
import jax
import jax.numpy as jnp
from jax import lax

D = 768
HEADS = 12
HD = 64
FF = 3072
SEQ = 197
SLOTS = 6
MB = 2
RANKS = 16
IMAGES = 96
N_TENSOR = 2


def draw_live_images(key, part):
    first_key, second_key = jax.random.split(jax.random.fold_in(key, 11))
    counts = jax.random.randint(first_key, (MB, RANKS), 1, SLOTS + 1)
    fullest = jax.random.randint(second_key, (MB, 1), 0, RANKS)
    lonely = (fullest + RANKS // 2) % RANKS
    rank_ids = jnp.arange(RANKS)[None, :]
    counts = jnp.where(rank_ids == fullest, SLOTS, counts)
    counts = jnp.where(rank_ids == lonely, 1, counts)
    return counts.astype(jnp.int32)


def draw_qkv_weight(key, part):
    first_key = jax.random.fold_in(jax.random.fold_in(key, 23), 0)
    scale = D ** (-0.5)
    drawn = jax.random.truncated_normal(first_key, -4.0, 4.0, (D, 3, D), jnp.float32) * scale
    return jnp.clip(drawn, -1.0, 1.0).astype(jnp.bfloat16)


def spiked(values, own_key, source, target, blocks, factor):
    owner, partner = [(jnp.arange(values.shape[axis_at]) // (values.shape[axis_at] // blocks)).reshape([-1 if axis == axis_at else 1 for axis in range(values.ndim)]) for axis_at in (source, target)]
    chosen = jax.random.permutation(own_key, blocks)[partner]
    strong = (owner == chosen) | (owner == (partner + blocks // 2) % blocks)
    return jnp.where(strong, factor * values, values)


def shard_levels(own_key, shape, cuts, low, top_value):
    def one(axis_at, parts):
        draws = jax.random.uniform(jax.random.fold_in(jax.random.fold_in(own_key, 6), axis_at), (parts,), jnp.float32, low / len(cuts), top_value / len(cuts))
        return jnp.repeat(jnp.exp(draws), shape[axis_at] // parts).reshape((-1,) + (1,) * (len(shape) - axis_at - 1))

    level = one(*cuts[0])
    for cut in cuts[1:]:
        level = level * one(*cut)
    return level


def gaussian(own_key, shape, deviation, limit, cuts=(), dtype=jnp.bfloat16):
    level = shard_levels(own_key, shape, cuts, -0.22, 0.18) if cuts else 1.0
    entries = jax.random.normal(own_key, shape, jnp.float32) * deviation * level
    return jnp.minimum(jnp.maximum(entries, -limit), limit).astype(dtype)


def noise_with(key, extent, deviation, limit, shards, heavy, held_as=jnp.bfloat16):
    entries = deviation * jax.random.normal(key, extent, jnp.float32)
    if shards:
        entries = entries * shard_levels(key, extent, shards, -0.22, 0.18)
    return jnp.clip(spiked(entries, jax.random.fold_in(key, 3), *heavy), -limit, limit).astype(held_as)


def setup_inputs(seed: int = 0) -> dict:
    streams_of = jax.random.split(jax.random.key(seed), 16)
    return {
        "images": gaussian(streams_of[0], (MB, IMAGES, SEQ, D), 1.0, 6.0, ((1, 16),)),
        "live_images": draw_live_images(jax.random.fold_in(streams_of[15], 71), 0),
        "ln1_gain": jnp.clip(1.0 + 0.1 * jax.random.normal(streams_of[2], (D,), jnp.float32), 0.5, 1.5).astype(jnp.bfloat16),
        "ln1_bias": gaussian(streams_of[3], (D,), 0.5, 3.0, ((0, 16),)),
        "qkv_weight": draw_qkv_weight(jax.random.fold_in(streams_of[15], 71), 0),
        "qkv_bias": gaussian(streams_of[5], (2, D), 0.5, 3.0, ((1, 32),)),
        "proj_weight": gaussian(streams_of[6], (D, D), (D // 16) ** -0.5, 0.875, ((0, 2), (1, 16))),
        "proj_bias": gaussian(streams_of[7], (D,), 0.5, 3.0, ((0, 16),)),
        "ln2_gain": jnp.clip(1.0 + 0.1 * jax.random.normal(streams_of[8], (D,), jnp.float32), 0.5, 1.5).astype(jnp.bfloat16),
        "ln2_bias": gaussian(streams_of[9], (D,), 0.5, 3.0, ((0, 16),)),
        "fc1_weight": gaussian(streams_of[10], (D, FF), D ** -0.5, 0.21875, ((0, 16), (1, 2))),
        "fc1_bias": gaussian(streams_of[11], (FF,), 0.5, 3.0, ((0, 32),)),
        "fc2_weight": gaussian(streams_of[12], (FF, D), FF ** -0.5, 0.109375, ((0, 2), (1, 16))),
        "fc2_bias": gaussian(streams_of[13], (D,), 0.5, 3.0, ((0, 16),)),
        "cotangent": noise_with(streams_of[14], (MB, IMAGES, SEQ, D), 1.0, 6.0, ((1, 16),), (1, 3, 16, 2.0)),
    }


eps = 1e-06

def layer_norm(values, gain, shift):
    center = lax.optimization_barrier(jnp.mean(values, axis=-1, keepdims=True))
    offset = values - center
    variance = lax.optimization_barrier(jnp.mean(offset * offset, axis=-1, keepdims=True))
    inverse = lax.rsqrt(variance + eps)
    scaled = offset * inverse
    return (scaled * gain + shift, scaled, inverse)

def norm_back(grad_norm, scaled, inverse, gain):
    weighted = grad_norm * gain
    first_mean = lax.optimization_barrier(jnp.mean(weighted, axis=-1, keepdims=True))
    second_mean = lax.optimization_barrier(jnp.mean(weighted * scaled, axis=-1, keepdims=True))
    return inverse * (weighted - first_mean - scaled * second_mean)

def gelu_exact(values):
    return jax.nn.gelu(values, approximate=False)

def round_sum(partials):
    rounded = lax.optimization_barrier(partials.astype(jnp.bfloat16))
    return lax.optimization_barrier(jnp.sum(rounded.astype(jnp.float32), axis=0))

def group_parts(operand, factor, groups):
    row_count = operand.shape[0]
    inner_size = operand.shape[1] // groups
    partials = jnp.einsum('rtc,tcd->trd', operand.reshape(row_count, groups, inner_size).astype(jnp.float32), factor.reshape(groups, inner_size, factor.shape[1]).astype(jnp.float32))
    return round_sum(partials)

def inner_rows(operand, factor):
    return lax.dot_general(operand, factor, (((0,), (0,)), ((), ())), preferred_element_type=jnp.float32)

def outer_cols(operand, factor):
    return lax.dot_general(operand, factor, (((1,), (1,)), ((), ())), preferred_element_type=jnp.float32)

def reference(images, live_images, ln1_gain, ln1_bias, qkv_weight, qkv_bias, proj_weight, proj_bias, ln2_gain, ln2_bias, fc1_weight, fc1_bias, fc2_weight, fc2_bias, cotangent):
    scale = HD ** (-0.5)
    row_count = SLOTS * SEQ
    head_cols = D // N_TENSOR
    picture_groups = images.reshape(MB * RANKS, SLOTS, SEQ, D)
    upstream_groups = cotangent.reshape(MB * RANKS, SLOTS, SEQ, D)
    slot_ids = jnp.arange(SLOTS).astype(jnp.int32)
    alive_groups = (slot_ids[None, None, :] < live_images[:, :, None].astype(jnp.int32)).astype(jnp.float32)
    alive_groups = alive_groups.reshape(MB * RANKS, SLOTS)
    gain_one = ln1_gain.astype(jnp.float32)
    shift_one = ln1_bias.astype(jnp.float32)
    gain_two = ln2_gain.astype(jnp.float32)
    shift_two = ln2_bias.astype(jnp.float32)
    bias_full = jnp.stack([qkv_bias[0], jnp.zeros_like(qkv_bias[0]), qkv_bias[1]]).astype(jnp.float32)
    flat_qkv = qkv_weight.reshape(D, 3 * D)

    def one_group(carry, inputs):
        picture, alive_slots, upstream = inputs
        alive_rows = jnp.broadcast_to(alive_slots[:, None, None], (SLOTS, SEQ, 1)).reshape(row_count, 1)
        inputs_f = picture.astype(jnp.float32).reshape(row_count, D)
        normed_one, scaled_one, inverse_one = layer_norm(inputs_f, gain_one, shift_one)
        normed_one = normed_one.astype(jnp.bfloat16)
        mixed = jnp.dot(normed_one, flat_qkv, preferred_element_type=jnp.float32).reshape(row_count, 3, D)
        mixed = (mixed + bias_full).astype(jnp.bfloat16)
        query = mixed[:, 0].reshape(SLOTS, SEQ, HEADS, HD)
        keys_all = mixed[:, 1].reshape(SLOTS, SEQ, HEADS, HD)
        values_all = mixed[:, 2].reshape(SLOTS, SEQ, HEADS, HD)
        scores = jnp.einsum('gqhe,gkhe->ghqk', query.astype(jnp.float32), keys_all.astype(jnp.float32)) * scale
        log_total = jax.nn.logsumexp(scores, axis=-1)
        weights = jnp.exp(scores - log_total[..., None])
        probs = weights.astype(jnp.bfloat16)
        context = jnp.einsum('ghqk,gkhe->gqhe', probs.astype(jnp.float32), values_all.astype(jnp.float32))
        context = context.astype(jnp.bfloat16).reshape(row_count, D)
        resid_one = inputs_f + group_parts(context, proj_weight, N_TENSOR) + proj_bias.astype(jnp.float32)
        normed_two, scaled_two, inverse_two = layer_norm(resid_one, gain_two, shift_two)
        normed_two = normed_two.astype(jnp.bfloat16)
        before = jnp.dot(normed_two, fc1_weight, preferred_element_type=jnp.float32) + fc1_bias.astype(jnp.float32)
        hidden = gelu_exact(before).astype(jnp.bfloat16)
        result = (resid_one + group_parts(hidden, fc2_weight, N_TENSOR) + fc2_bias.astype(jnp.float32)) * alive_rows
        activ = result.astype(jnp.bfloat16).reshape(SLOTS, SEQ, D)
        grad_out = upstream.astype(jnp.float32).reshape(row_count, D) * alive_rows
        grad_out_b = grad_out.astype(jnp.bfloat16)
        delta_fc2_bias = lax.optimization_barrier(jnp.sum(grad_out, axis=0))
        delta_fc2_weight = inner_rows(hidden, grad_out_b)
        grad_hidden = outer_cols(grad_out_b, fc2_weight)
        grad_before = jax.vjp(gelu_exact, before)[1](grad_hidden)[0]
        grad_before_b = grad_before.astype(jnp.bfloat16)
        delta_fc1_bias = lax.optimization_barrier(jnp.sum(grad_before, axis=0))
        delta_fc1_weight = inner_rows(normed_two, grad_before_b)
        grad_norm_two = group_parts(grad_before_b, fc1_weight.T, N_TENSOR)
        delta_gain_two = lax.optimization_barrier(jnp.sum(grad_norm_two * scaled_two, axis=0))
        delta_shift_two = lax.optimization_barrier(jnp.sum(grad_norm_two, axis=0))
        grad_resid = grad_out + norm_back(grad_norm_two, scaled_two, inverse_two, gain_two)
        delta_proj_bias = lax.optimization_barrier(jnp.sum(grad_resid, axis=0))
        grad_resid_b = grad_resid.astype(jnp.bfloat16)
        delta_proj_weight = inner_rows(context, grad_resid_b)
        grad_context = outer_cols(grad_resid_b, proj_weight).astype(jnp.bfloat16).reshape(SLOTS, SEQ, HEADS, HD)
        again = jnp.einsum('gqhe,gkhe->ghqk', query.astype(jnp.float32), keys_all.astype(jnp.float32)) * scale
        weights_again = jnp.exp(again - log_total[..., None])
        probs_again = weights_again.astype(jnp.bfloat16)
        grad_probs = jnp.einsum('gqhe,gkhe->ghqk', grad_context.astype(jnp.float32), values_all.astype(jnp.float32))
        row_dot = lax.optimization_barrier(jnp.sum(weights_again * grad_probs, axis=-1, keepdims=True))
        grad_scores = (weights_again * (grad_probs - row_dot) * scale).astype(jnp.bfloat16).astype(jnp.float32)
        grad_query = jnp.einsum('ghqk,gkhe->gqhe', grad_scores, keys_all.astype(jnp.float32))
        grad_keys = jnp.einsum('ghqk,gqhe->gkhe', grad_scores, query.astype(jnp.float32))
        grad_values = jnp.einsum('ghqk,gqhe->gkhe', probs_again.astype(jnp.float32), grad_context.astype(jnp.float32))
        grad_mixed = jnp.stack([grad_query.reshape(row_count, D), grad_keys.reshape(row_count, D), grad_values.reshape(row_count, D)], axis=1)
        delta_qkv_bias = jnp.stack([lax.optimization_barrier(jnp.sum(grad_mixed[:, 0], axis=0)), lax.optimization_barrier(jnp.sum(grad_mixed[:, 2], axis=0))])
        grad_mixed_b = grad_mixed.astype(jnp.bfloat16)
        delta_qkv_weight = inner_rows(normed_one, grad_mixed_b.reshape(row_count, 3 * D)).reshape(D, 3, D)
        partials = jnp.einsum('rcth,dcth->trd', grad_mixed_b.reshape(row_count, 3, N_TENSOR, head_cols).astype(jnp.float32), qkv_weight.reshape(D, 3, N_TENSOR, head_cols).astype(jnp.float32))
        grad_norm_one = round_sum(partials)
        delta_gain_one = lax.optimization_barrier(jnp.sum(grad_norm_one * scaled_one, axis=0))
        delta_shift_one = lax.optimization_barrier(jnp.sum(grad_norm_one, axis=0))
        grad_input = grad_resid + norm_back(grad_norm_one, scaled_one, inverse_one, gain_one)
        terms = (delta_gain_one, delta_shift_one, delta_qkv_weight, delta_qkv_bias, delta_proj_weight, delta_proj_bias, delta_gain_two, delta_shift_two, delta_fc1_weight, delta_fc1_bias, delta_fc2_weight, delta_fc2_bias)
        carry = jax.tree.map(lambda total, term: total + term, carry, terms)
        return (carry, (activ, grad_input.reshape(SLOTS, SEQ, D)))
    zeros_d = jnp.zeros((D,), jnp.float32)
    start = (zeros_d, zeros_d, jnp.zeros((D, 3, D), jnp.float32), jnp.zeros((2, D), jnp.float32), jnp.zeros((D, D), jnp.float32), zeros_d, zeros_d, zeros_d, jnp.zeros((D, FF), jnp.float32), jnp.zeros((FF,), jnp.float32), jnp.zeros((FF, D), jnp.float32), zeros_d)
    final, (activ_all, grads_all) = lax.scan(one_group, start, (picture_groups, alive_groups, upstream_groups))
    return (activ_all.reshape(MB, IMAGES, SEQ, D), grads_all.reshape(MB, IMAGES, SEQ, D), final[0], final[1], final[2], final[3], final[4], final[5], final[6], final[7], final[8], final[9], final[10], final[11])
```

```python
import functools
import math

import jax
import jax.numpy as jnp
from jax import lax
from jax.experimental import pallas as pl
from jax.experimental.pallas import tpu as pltpu
from jax.sharding import PartitionSpec as P

HD = 64
EPS = 1e-06
BF = jnp.bfloat16
F32 = jnp.float32
ROW_TILE = 16
LANES = 128
BATCH = 2
CHUNKS = 3
VMEM_LIMIT = 60 * 1024 * 1024

ERFC = (
    0.16918800397535036,
    0.17071524523359413,
    0.14833905737234418,
    0.21492644132531408,
    -0.09465150833103098,
    0.5477210173469333,
    -0.5122788444212757,
    0.4855635302821805,
    -0.1295229623684681,
)
ERFC_HALF = tuple(0.5 * c for c in ERFC)
T_SCALE = 0.3 / math.sqrt(2.0)
PHI_SCALE = 1.0 / math.sqrt(2.0 * math.pi)


def gelu_pair(v):
    t = 1.0 / (1.0 + T_SCALE * jnp.abs(v))
    acc = jnp.full_like(v, ERFC_HALF[-1])
    for c in ERFC_HALF[-2::-1]:
        acc = acc * t + c
    e = jnp.exp(-0.5 * v * v)
    tail = acc * t * e
    cdf = jnp.where(v >= 0, 1.0 - tail, tail)
    return v * cdf, cdf + v * (PHI_SCALE * e)


def nt(a, b):
    return lax.dot_general(a, b, (((1,), (1,)), ((), ())), preferred_element_type=F32)


def tn(a, b):
    return lax.dot_general(a, b, (((0,), (0,)), ((), ())), preferred_element_type=F32)


def nn(a, b):
    return jnp.dot(a, b, preferred_element_type=F32)


def norm_stats(x):
    center = jnp.mean(x, axis=-1, keepdims=True)
    offset = x - center
    inverse = lax.rsqrt(jnp.mean(offset * offset, axis=-1, keepdims=True) + EPS)
    return offset * inverse, inverse


def norm_back(g, scaled, inverse, gain):
    u = g * gain
    first = jnp.mean(u, axis=-1, keepdims=True)
    second = jnp.mean(u * scaled, axis=-1, keepdims=True)
    return inverse * (u - first - scaled * second)


def fold8(x):
    return jnp.sum(x.reshape(x.shape[0] // 8, 8, x.shape[1]), axis=0)


def add_to(ref, value):
    @pl.when(pl.program_id(0) == 0)
    def _():
        ref[...] = value

    @pl.when(pl.program_id(0) > 0)
    def _():
        ref[...] += value


def load_weights(table, sources, w, sem):
    copies = []
    k = 0
    cols = w.shape[1] // len(sources)
    for h, arrays in enumerate(sources):
        for src in arrays:
            blocks, rows, _ = src.shape
            for s in range(blocks):
                row = pl.multiple_of(table[k] * rows, ROW_TILE)
                copies.append(
                    pltpu.make_async_copy(
                        src.at[s], w.at[pl.ds(row, rows), pl.ds(h * cols, cols)], sem.at[k]
                    )
                )
                k += 1
    return copies


def split_sources(refs, per_half):
    return refs[:per_half], refs[per_half : 2 * per_half]


def attn_fwd_kernel(seq, per_half, table, x_ref, vec_ref, *refs):
    sources = split_sources(refs, per_half)
    normed_ref, qkv_ref, lse_ref, ctx_ref, w, sem = refs[2 * per_half :]
    copies = load_weights(table, sources, w, sem)
    first = pl.program_id(0) == 0

    @pl.when(first)
    def _():
        for c in copies:
            c.start()

    width = x_ref.shape[1]
    cols = qkv_ref.shape[2]
    group = cols // 3
    scaled, _ = norm_stats(x_ref[...].astype(F32))
    normed = (scaled * vec_ref[0:1, :width] + vec_ref[1:2, :width]).astype(BF)
    normed_ref[...] = normed

    @pl.when(first)
    def _():
        for c in copies:
            c.wait()

    for h in range(2):
        part = nn(normed, w[:, h * cols : (h + 1) * cols]) + vec_ref[7:8, h * cols : (h + 1) * cols]
        qkv_ref[h] = part.astype(BF)

    tall = x_ref.shape[0] // BATCH
    lane = lax.broadcasted_iota(jnp.int32, (tall, LANES), 1)
    low = lane < HD
    keep = lax.broadcasted_iota(jnp.int32, (tall, tall), 1) < seq

    def one(step, carry):
        image, h = step // 2, step % 2
        rows = pl.ds(pl.multiple_of(image * tall, ROW_TILE), tall)
        logs = jnp.zeros((tall, LANES), F32)
        for pair in range(group // LANES):
            at = pair * LANES
            q = qkv_ref[h, rows, at : at + LANES] * 0.125
            k = qkv_ref[h, rows, group + at : group + at + LANES]
            v = qkv_ref[h, rows, 2 * group + at : 2 * group + at + LANES]
            outs = []
            for e in range(2):
                mine = low if e == 0 else ~low
                s = nt(jnp.where(mine, q, jnp.zeros_like(q)), k)
                s = jnp.where(keep, s, -1e30)
                top = jnp.max(s, axis=-1, keepdims=True)
                p = jnp.exp(s - top)
                total = jnp.sum(p, axis=-1, keepdims=True)
                logs = jnp.where(lane == 2 * pair + e, top + jnp.log(total), logs)
                probs = (p * (1.0 / total)).astype(BF)
                outs.append(nn(probs, v))
            ctx_ref[h, rows, at : at + LANES] = jnp.where(low, outs[0], outs[1]).astype(BF)
        lse_ref[h, rows, :] = logs
        return carry

    lax.fori_loop(0, 2 * BATCH, one, 0)


def mlp_fwd_kernel(per_half, table, live, ctx_ref, x_ref, vec_ref, *refs):
    sources = split_sources(refs, per_half)
    resid_ref, normed_ref, hidden_ref, slope_ref, act_ref, w, sem, acc = refs[2 * per_half :]
    copies = load_weights(table, sources, w, sem)
    step = pl.program_id(0)

    @pl.when(step == 0)
    def _():
        for c in copies:
            c.start()
        for c in copies:
            c.wait()

    rows, width = x_ref.shape
    cols = w.shape[1] // 2
    group, ff = ctx_ref.shape[2], hidden_ref.shape[2]
    attn = nt(ctx_ref[0], w[:, :group]) + nt(ctx_ref[1], w[:, cols : cols + group])
    resid = x_ref[...].astype(F32) + attn + vec_ref[2:3, :width]
    resid_ref[...] = resid
    scaled, _ = norm_stats(resid)
    normed_ref[...] = (scaled * vec_ref[3:4, :width] + vec_ref[4:5, :width]).astype(BF)
    chunk = ff // CHUNKS

    def one(step, carry):
        h, c = step // CHUNKS, step % CHUNKS
        at = pl.multiple_of(h * cols + group + c * chunk, LANES)
        here = pl.ds(pl.multiple_of(c * chunk, LANES), chunk)
        bias = vec_ref[6:7, pl.ds(pl.multiple_of(step * chunk, LANES), chunk)]
        value, slope = gelu_pair(nn(normed_ref[...], w[:, pl.ds(at, chunk)]) + bias)
        hidden = value.astype(BF)
        hidden_ref[h, :, here] = hidden
        slope_ref[h, :, here] = slope.astype(BF)
        acc[...] += nt(hidden, w[:, pl.ds(pl.multiple_of(at + ff, LANES), chunk)])
        return carry

    acc[...] = resid
    lax.fori_loop(0, 2 * CHUNKS, one, 0)
    image = lax.broadcasted_iota(jnp.int32, (rows, 1), 0) // (rows // BATCH)
    alive = jnp.zeros((rows, 1), F32)
    for i in range(BATCH):
        alive = jnp.where(image == i, live[step * BATCH + i].astype(F32), alive)
    act_ref[...] = ((acc[...] + vec_ref[5:6, :width]) * alive).astype(BF)


def mlp_bwd_kernel(per_half, table, go_ref, slope_ref, resid_ref, vec_ref, *refs):
    sources = split_sources(refs, per_half)
    gpre_ref, gr_ref, grb_ref, gctx_ref, small_ref, fc1b_ref, w, sem = refs[2 * per_half :]
    copies = load_weights(table, sources, w, sem)
    step = pl.program_id(0)

    @pl.when(step == 0)
    def _():
        fc1b_ref[...] = jnp.zeros_like(fc1b_ref)
        for c in copies:
            c.start()
        for c in copies:
            c.wait()

    rows, width = go_ref.shape
    cols = w.shape[1] // 2
    group, ff = gctx_ref.shape[2], gpre_ref.shape[2]
    chunk = ff // 3

    def one(h, acc):
        for c in range(3):
            at = pl.multiple_of(h * cols + group + c * chunk, LANES)
            gh = nn(go_ref[...], w[:, pl.ds(pl.multiple_of(at + ff, LANES), chunk)])
            gpre = gh * slope_ref[h, :, c * chunk : (c + 1) * chunk].astype(F32)
            where = pl.ds(pl.multiple_of(h * ff + c * chunk, LANES), chunk)
            fc1b_ref[:, where] += fold8(gpre)
            gpre = gpre.astype(BF)
            gpre_ref[h, :, c * chunk : (c + 1) * chunk] = gpre
            acc = acc + nt(gpre, w[:, pl.ds(at, chunk)])
        return acc

    gn = lax.fori_loop(0, 2, one, jnp.zeros((rows, width), F32))
    scaled, inverse = norm_stats(resid_ref[...])
    go = go_ref[...].astype(F32)
    gr = go + norm_back(gn, scaled, inverse, vec_ref[3:4, :width])
    gr_ref[...] = gr
    grb = gr.astype(BF)
    grb_ref[...] = grb
    for h in range(2):
        gctx_ref[h] = nn(grb, w[:, h * cols : h * cols + group]).astype(BF)
    add_to(
        small_ref,
        jnp.concatenate([fold8(gn * scaled), fold8(gn), fold8(gr), fold8(go)], axis=0),
    )


def attn_bwd_kernel(seq, per_half, table, qkv_ref, lse_ref, gctx_ref, x_ref, gr_ref, vec_ref, *refs):
    sources = split_sources(refs, per_half)
    gqkv_ref, gin_ref, small_ref, bias_ref, w, sem = refs[2 * per_half :]
    copies = load_weights(table, sources, w, sem)
    first = pl.program_id(0) == 0

    @pl.when(first)
    def _():
        bias_ref[...] = jnp.zeros_like(bias_ref)
        for c in copies:
            c.start()

    rows, width = x_ref.shape
    cols = qkv_ref.shape[2]
    group = cols // 3
    tall = rows // BATCH
    lane = lax.broadcasted_iota(jnp.int32, (tall, LANES), 1)
    low = lane < HD
    keep = lax.broadcasted_iota(jnp.int32, (tall, tall), 1) < seq

    pairs = group // LANES

    def one(step, carry):
        image, h, pair = step // (2 * pairs), step // pairs % 2, step % pairs
        at_rows = pl.ds(pl.multiple_of(image * tall, ROW_TILE), tall)
        at = pair * LANES
        cols_of = [pl.ds(pl.multiple_of(part * group + at, LANES), LANES) for part in range(3)]
        logs = lse_ref[h, at_rows, :]
        q = qkv_ref[h, at_rows, cols_of[0]] * 0.125
        k = qkv_ref[h, at_rows, cols_of[1]]
        v = qkv_ref[h, at_rows, cols_of[2]]
        g = gctx_ref[h, at_rows, cols_of[0]]
        got = []
        for e in range(2):
            mine = low if e == 0 else ~low
            s = nt(jnp.where(mine, q, jnp.zeros_like(q)), k)
            lse = jnp.sum(jnp.where(lane == 2 * pair + e, logs, 0.0), axis=-1, keepdims=True)
            weights = jnp.exp(jnp.where(keep, s - lse, -1e30))
            gp = nt(jnp.where(mine, g, jnp.zeros_like(g)), v)
            wg = weights * gp
            dot = jnp.sum(wg, axis=-1, keepdims=True)
            gs = (wg - weights * dot).astype(BF)
            got.append((nn(gs, k), tn(gs, q), tn(weights.astype(BF), g)))
        gq, gk, gv = (jnp.where(low, a, b) for a, b in zip(*got))
        gq = gq * 0.125
        for to, value in zip(cols_of, (gq, gk, gv)):
            gqkv_ref[h, at_rows, to] = value.astype(BF)
        bias_ref[h, 0:8, cols_of[0]] += fold8(gq)
        bias_ref[h, 8:16, cols_of[0]] += fold8(gv)
        return carry

    lax.fori_loop(0, 2 * BATCH * pairs, one, 0)

    @pl.when(first)
    def _():
        for c in copies:
            c.wait()

    gn = nt(gqkv_ref[0], w[:, :cols]) + nt(gqkv_ref[1], w[:, cols:])
    scaled, inverse = norm_stats(x_ref[...].astype(F32))
    gin = gr_ref[...] + norm_back(gn, scaled, inverse, vec_ref[0:1, :width])
    gin_ref[...] = gin.astype(BF)
    add_to(small_ref, jnp.concatenate([fold8(gn * scaled), fold8(gn)], axis=0))


SMEM_SPEC = pl.BlockSpec(memory_space=pltpu.SMEM)
ANY_SPEC = pl.BlockSpec(memory_space=pl.ANY)


def row_spec(step_rows, shape):
    if len(shape) == 2:
        return pl.BlockSpec((step_rows, shape[1]), lambda i: (i, 0))
    return pl.BlockSpec((shape[0], step_rows, shape[2]), lambda i: (0, i, 0))


def whole_spec(shape):
    return pl.BlockSpec(shape, lambda i: (0,) * len(shape))


def run(kernel, name, steps, step_rows, scalars, rows_in, whole_in, sources, rows_out, whole_out, w_cols, flops, extra=()):
    flat = [a for half in sources for a in half]
    n_copies = sum(a.shape[0] for a in flat)
    width = sum(a.shape[0] * a.shape[1] for a in sources[0])
    out_shape = [jax.ShapeDtypeStruct(s, d) for s, d in rows_out + whole_out]
    moved = sum(a.size * a.dtype.itemsize for a in rows_in + flat)
    moved += sum(math.prod(s) * jnp.dtype(d).itemsize for s, d in rows_out)
    return pl.pallas_call(
        kernel,
        name=name,
        grid=(steps,),
        in_specs=[SMEM_SPEC] * len(scalars)
        + [row_spec(step_rows, a.shape) for a in rows_in]
        + [whole_spec(a.shape) for a in whole_in]
        + [ANY_SPEC] * len(flat),
        out_specs=[row_spec(step_rows, s) for s, _ in rows_out] + [whole_spec(s) for s, _ in whole_out],
        out_shape=out_shape,
        scratch_shapes=[pltpu.VMEM((width, w_cols), BF), pltpu.SemaphoreType.DMA((n_copies,)), *extra],
        compiler_params=pltpu.CompilerParams(
            dimension_semantics=("arbitrary",), vmem_limit_bytes=VMEM_LIMIT
        ),
        cost_estimate=pl.CostEstimate(flops=flops, bytes_accessed=moved, transcendentals=0),
    )(*scalars, *rows_in, *whole_in, *flat)


class Links:
    def __init__(self, n_dp, n_t, width):
        self.n_dp, self.n_t = n_dp, n_t
        self.rows = width // n_dp
        self.fast = n_dp % 4 == 0 and n_dp & (n_dp - 1) == 0 and self.rows % ROW_TILE == 0
        self.d = lax.axis_index("dp")
        self.t = lax.axis_index("tensor")
        self.nz = n_dp // 4
        self.x, self.y, self.z = self.d % 2, (self.d // 2) % 2, self.d // 4
        n = n_dp * n_t

        def joint(move):
            return [(i, move(i // n_t, i % n_t)) for i in range(n)]

        self.first = joint(lambda d, t: (d ^ (1 if t == 0 else 2)) * n_t + t)
        self.second = joint(lambda d, t: (d ^ (2 if t == 0 else 1)) * n_t + t)
        self.shift = [
            [(i, (i + 4 * j) % n_dp) for i in range(n_dp)] for j in range(self.nz)
        ]
        self.bits = [
            [(i, i ^ (1 << b)) for i in range(n)] for b in range((n - 1).bit_length())
        ]
        self.swap = [(i, i ^ 1) for i in range(n_t)]

    def partner(self, a):
        return lax.ppermute(a, "tensor", self.swap)

    def step(self, a, perm):
        return lax.ppermute(a, ("dp", "tensor"), perm)

    def gather(self, p):
        if not self.fast:
            own = lax.all_gather(p, "dp", axis=0, tiled=True)[None]
            return (own,), (self.partner(own),)
        a = jnp.stack([p] + [lax.ppermute(p, "dp", s) for s in self.shift[1:]])
        a = jnp.concatenate([a, self.step(a, self.first)])
        b = self.step(a, self.second)
        return (a, b), (self.partner(a), self.partner(b))

    def table(self):
        if not self.fast:
            return jnp.zeros((2,), jnp.int32)
        h, s3, s2, j = (
            v.reshape(-1) for v in jnp.meshgrid(*(jnp.arange(k) for k in (2, 2, 2, self.nz)), indexing="ij")
        )
        zero = (self.t ^ h) == 0
        x = self.x ^ jnp.where(zero, s2, s3)
        y = self.y ^ jnp.where(zero, s3, s2)
        z = (self.z - j + self.nz) % self.nz
        return ((z * 2 + y) * 2 + x).astype(jnp.int32)

    def scatter(self, g):
        if not self.fast:
            return lax.psum_scatter(g.astype(F32), "dp", scatter_dimension=0, tiled=True)
        v = g.reshape(self.nz, 2, 2, self.rows, g.shape[1])

        def pick(a, axis, at):
            return lax.dynamic_index_in_dim(a, at, axis, keepdims=False)

        zero = self.t == 0
        send = jnp.where(zero, pick(v, 1, 1 - self.y), pick(v, 2, 1 - self.x))
        held = jnp.where(zero, pick(v, 1, self.y), pick(v, 2, self.x))
        got = self.step(send, self.second)
        held = (held.astype(F32) + got.astype(F32)).astype(BF)
        mine = jnp.where(zero, self.x, self.y)
        got = self.step(pick(held, 1, 1 - mine), self.first)
        held = (pick(held, 1, mine).astype(F32) + got.astype(F32)).astype(BF)
        total = pick(held, 0, self.z).astype(F32)
        for j in range(1, self.nz):
            out = pick(held, 0, (self.z + j) % self.nz)
            total = total + lax.ppermute(out, "dp", self.shift[j]).astype(F32)
        return total

    def total(self, a):
        if not self.fast:
            return lax.psum(a, ("dp", "tensor"))
        for perm in self.bits:
            a = a + self.step(a, perm)
        return a


def weight_grad(links, a, b):
    away = links.partner(tn(a, b[1]).astype(BF))
    return (tn(a, b[0]) + away.astype(F32)).astype(BF)


def per_device(n_dp, n_t, *args):
    (
        images,
        live_images,
        ln1_gain,
        ln1_bias,
        qkv_weight,
        qkv_bias,
        proj_weight,
        proj_bias,
        ln2_gain,
        ln2_bias,
        fc1_weight,
        fc1_bias,
        fc2_weight,
        fc2_bias,
        cotangent,
    ) = args
    micro, slots, seq, _ = images.shape
    width = proj_weight.shape[1] * n_dp
    group = proj_weight.shape[0]
    ff = fc1_weight.shape[1]
    links = Links(n_dp, n_t, width)
    t, rows = links.t, links.rows
    count = micro * slots // n_t
    tall = -(-seq // ROW_TILE) * ROW_TILE
    total_rows = count * tall
    steps = count // BATCH
    step_rows = BATCH * tall

    qkv_shard = qkv_weight.reshape(rows, 3 * group)
    rest_shard = jnp.concatenate([proj_weight.T, fc1_weight, fc2_weight.T], axis=1)
    vectors = [ln1_gain, ln1_bias, proj_bias, ln2_gain, ln2_bias, fc2_bias]
    own_small = jnp.concatenate(vectors + [qkv_bias.reshape(-1), fc1_bias]).astype(F32)
    n_small = own_small.shape[0]
    board = jnp.zeros((n_dp * n_t, n_small), F32)
    board = lax.dynamic_update_slice(board, own_small[None], (links.d * n_t + t, 0))
    board = links.total(board).reshape(n_dp, n_t, n_small)
    qkv_src = links.gather(qkv_shard)
    rest_src = links.gather(rest_shard)
    table = links.table()

    n_vec = len(vectors) * rows
    six = board[:, 0, :n_vec].reshape(n_dp, len(vectors), rows).transpose(1, 0, 2)
    six = six.reshape(len(vectors), width)

    def own_first(a):
        return jnp.where(t == 0, a, a[::-1])

    qb = board[:, :, n_vec : n_vec + qkv_bias.size].reshape(n_dp, n_t, 2, qkv_bias.shape[1])
    qb = qb.transpose(1, 2, 0, 3).reshape(n_t, 2, group)
    qb = jnp.stack([qb[:, 0], jnp.zeros_like(qb[:, 0]), qb[:, 1]], axis=1)
    qb = own_first(qb.reshape(n_t, 3 * group)).reshape(1, -1)
    fb = board[:, :, n_vec + qkv_bias.size :].transpose(1, 0, 2).reshape(n_t, ff)
    fb = own_first(fb).reshape(1, -1)

    def wide(a):
        return jnp.pad(a, ((0, 0), (0, n_t * ff - a.shape[1])))

    vec = jnp.concatenate([wide(six), fb, wide(qb)])

    def mine(a):
        a = a.reshape(micro * slots, seq, width)
        return lax.dynamic_slice_in_dim(a, t * count, count, 0)

    def padded(a):
        return jnp.pad(a, ((0, 0), (0, tall - seq), (0, 0))).reshape(total_rows, width)

    alive = (jnp.arange(slots)[None, :] < live_images).astype(jnp.int32).reshape(-1)
    live = lax.dynamic_slice_in_dim(alive, t * count, count, 0)
    x = padded(mine(images))
    go = padded(mine(cotangent) * live[:, None, None].astype(BF))

    per_half = len(qkv_src[0])
    base = 2 * total_rows * width
    call = functools.partial(run, steps=steps, step_rows=step_rows)
    normed1, qkv, lse, ctx = call(
        functools.partial(attn_fwd_kernel, seq, per_half),
        "attn_fwd",
        scalars=[table],
        rows_in=[x],
        whole_in=[vec],
        sources=qkv_src,
        rows_out=[
            ((total_rows, width), BF),
            ((2, total_rows, 3 * group), BF),
            ((2, total_rows, LANES), F32),
            ((2, total_rows, group), BF),
        ],
        whole_out=[],
        w_cols=6 * group,
        flops=base * 8 * group,
    )
    rest_cols = 2 * rest_shard.shape[1]
    resid, normed2, hidden, slope, act = call(
        functools.partial(mlp_fwd_kernel, per_half),
        "mlp_fwd",
        scalars=[table, live],
        rows_in=[ctx, x],
        whole_in=[vec],
        sources=rest_src,
        rows_out=[
            ((total_rows, width), F32),
            ((total_rows, width), BF),
            ((2, total_rows, ff), BF),
            ((2, total_rows, ff), BF),
            ((total_rows, width), BF),
        ],
        whole_out=[],
        w_cols=rest_cols,
        flops=base * (2 * group + 4 * ff),
        extra=[pltpu.VMEM((step_rows, width), F32)],
    )
    act = act.reshape(count, tall, width)[:, :seq]
    act_away = links.partner(act)
    fc2_sum = links.scatter(weight_grad(links, go, hidden))
    gpre, gr, grb, gctx, small2, fc1b = call(
        functools.partial(mlp_bwd_kernel, per_half),
        "mlp_bwd",
        scalars=[table],
        rows_in=[go, slope, resid],
        whole_in=[vec],
        sources=rest_src,
        rows_out=[
            ((2, total_rows, ff), BF),
            ((total_rows, width), F32),
            ((total_rows, width), BF),
            ((2, total_rows, group), BF),
        ],
        whole_out=[((32, width), F32), ((8, 2 * ff), F32)],
        w_cols=rest_cols,
        flops=base * (2 * group + 4 * ff),
    )
    away = jnp.concatenate([tn(normed2, gpre[1]), tn(grb, ctx[1])], axis=1).astype(BF)
    away = links.partner(away).astype(F32)
    here = jnp.concatenate([tn(normed2, gpre[0]), tn(grb, ctx[0])], axis=1)
    mid_sum = links.scatter((here + away).astype(BF))
    gqkv, gin, small1, qkvb = call(
        functools.partial(attn_bwd_kernel, seq, per_half),
        "attn_bwd",
        scalars=[table],
        rows_in=[qkv, lse, gctx, x, gr],
        whole_in=[vec],
        sources=qkv_src,
        rows_out=[((2, total_rows, 3 * group), BF), ((total_rows, width), BF)],
        whole_out=[((16, width), F32), ((2, 16, group), F32)],
        w_cols=6 * group,
        flops=base * 8 * group,
    )
    gin = gin.reshape(count, tall, width)[:, :seq]
    gin_away = links.partner(gin)
    qkv_sum = links.scatter(weight_grad(links, normed1, gqkv))

    six_grads = jnp.sum(
        jnp.concatenate([small1.reshape(2, 8, width), small2.reshape(4, 8, width)]), axis=1
    )
    qb_grad = own_first(jnp.sum(qkvb.reshape(2, 2, 8, group), axis=2))
    fb_grad = own_first(jnp.sum(fc1b.reshape(8, 2, ff), axis=0))
    flat = jnp.concatenate([six_grads.reshape(-1), qb_grad.reshape(-1), fb_grad.reshape(-1)])
    flat = links.total(flat.reshape(-1, LANES)).reshape(-1)
    n_six = six_grads.size
    six_own = lax.dynamic_slice_in_dim(flat[:n_six].reshape(-1, width), links.d * rows, rows, 1)
    qb_all = flat[n_six : n_six + qb_grad.size].reshape(n_t, 2, n_dp, group // n_dp)
    qb_own = qb_all[t, :, links.d]
    fb_own = flat[n_six + qb_grad.size :].reshape(n_t, n_dp, ff // n_dp)[t, links.d]

    def joined(own, away):
        both = jnp.stack([jnp.where(t == 0, own, away), jnp.where(t == 0, away, own)])
        return both.reshape(micro, slots, seq, width)

    return (
        joined(act, act_away),
        joined(gin, gin_away).astype(F32),
        six_own[0],
        six_own[1],
        qkv_sum.reshape(rows, 3, group),
        qb_own,
        mid_sum[:, ff:].T,
        six_own[4],
        six_own[2],
        six_own[3],
        mid_sum[:, :ff],
        fb_own,
        fc2_sum.T,
        six_own[5],
    )


def solution(mesh):
    in_specs = (
        P(None, "dp", None, None),
        P(None, "dp"),
        P("dp"),
        P("dp"),
        P("dp", None, "tensor"),
        P(None, ("tensor", "dp")),
        P("tensor", "dp"),
        P("dp"),
        P("dp"),
        P("dp"),
        P("dp", "tensor"),
        P(("tensor", "dp")),
        P("tensor", "dp"),
        P("dp"),
        P(None, "dp", None, None),
    )
    out_specs = (
        P(None, "dp", None, None),
        P(None, "dp", None, None),
        P("dp"),
        P("dp"),
        P("dp", None, "tensor"),
        P(None, ("tensor", "dp")),
        P("tensor", "dp"),
        P("dp"),
        P("dp"),
        P("dp"),
        P("dp", "tensor"),
        P(("tensor", "dp")),
        P("tensor", "dp"),
        P("dp"),
    )
    body = functools.partial(per_device, mesh.shape["dp"], mesh.shape["tensor"])
    return jax.shard_map(body, mesh=mesh, in_specs=in_specs, out_specs=out_specs, check_vma=False)
```
